32 devices in a mesh: dp: 4 (over y, core), fsdp: 8 (over z, x).
Axes of the slice: x: 2, y: 2, z: 4, core: 2. Of those that a mesh axis runs over, the one named last changes fastest.
Arguments:
- hidden: bfloat16 [4096, 768], P(('dp', 'fsdp')), may hold values from -6 to 6
- memory: bfloat16 [8192, 768], P(('dp', 'fsdp')), may hold values from -6 to 6
- tgt_segments: int32 [4096], P(('dp', 'fsdp')), may hold values from 0 to 4, as said below
- mem_segments: int32 [8192], P(('dp', 'fsdp')), may hold values from 0 to 4, as said below
- labels: int32 [4096], P(('dp', 'fsdp')), may hold values from 0 to 32127
- self_query: bfloat16 [768, 768], P('fsdp', 'dp'), may hold values from -0.109375 to 0.109375
- self_key: bfloat16 [768, 768], P('fsdp', 'dp'), may hold values from -0.109375 to 0.109375
- self_value: bfloat16 [768, 768], P('fsdp', 'dp'), may hold values from -0.21875 to 0.21875
- self_out: bfloat16 [768, 768], P('fsdp', 'dp'), may hold values from -0.875 to 0.875
- cross_query: bfloat16 [768, 768], P('fsdp', 'dp'), may hold values from -0.109375 to 0.109375
- cross_key: bfloat16 [768, 768], P('fsdp', 'dp'), may hold values from -0.109375 to 0.109375
- cross_value: bfloat16 [768, 768], P('fsdp', 'dp'), may hold values from -0.21875 to 0.21875
- cross_out: bfloat16 [768, 768], P('fsdp', 'dp'), may hold values from -0.875 to 0.875
- gate_weight: bfloat16 [768, 2048], P('fsdp', 'dp'), may hold values from -0.21875 to 0.21875
- up_weight: bfloat16 [768, 2048], P('fsdp', 'dp'), may hold values from -0.21875 to 0.21875
- down_weight: bfloat16 [2048, 768], P('fsdp', 'dp'), may hold values from -0.25 to 0.25
- norm_gains: bfloat16 [3072], P(('dp', 'fsdp')), may hold values from 0.5 to 1.5
- embedding: bfloat16 [32128, 768], P('fsdp', 'dp'), may hold values from -12 to 12
Outputs:
- block_out: bfloat16 [4096, 768], P(('dp', 'fsdp'))
- loss_mean: float32 [], replicated
- grad_hidden: float32 [4096, 768], P(('dp', 'fsdp'))
- grad_memory: float32 [8192, 768], P(('dp', 'fsdp'))
- grad_self_query: float32 [768, 768], P('fsdp', 'dp')
- grad_self_key: float32 [768, 768], P('fsdp', 'dp')
- grad_self_value: float32 [768, 768], P('fsdp', 'dp')
- grad_self_out: float32 [768, 768], P('fsdp', 'dp')
- grad_cross_query: float32 [768, 768], P('fsdp', 'dp')
- grad_cross_key: float32 [768, 768], P('fsdp', 'dp')
- grad_cross_value: float32 [768, 768], P('fsdp', 'dp')
- grad_cross_out: float32 [768, 768], P('fsdp', 'dp')
- grad_gate: float32 [768, 2048], P('fsdp', 'dp')
- grad_up: float32 [768, 2048], P('fsdp', 'dp')
- grad_down: float32 [2048, 768], P('fsdp', 'dp')
- grad_gains: float32 [3072], P(('dp', 'fsdp'))
- grad_embedding: float32 [32128, 768], P('fsdp', 'dp')
The draws below stay inside these ranges and needn't reach their ends.
Inputs may be any that keep to these rules, and one draw needn't show every extreme that they name: `tgt_segments`: in each row of 128 target tokens the valid tokens come first and hold examples 1 to 4 in order, each non-empty; the row ends with one or more padding tokens marked 0. `mem_segments`: in each row of 256 memory tokens (row r serves target row r) the valid tokens come first and hold examples 1 to 4 in order, each non-empty; the row ends with one or more padding tokens marked 0.
All inputs are finite; a program needn't handle non-finite values.
Results may differ from the reference program's by a relative error of at most 0.03.
The reference program's roundings to bfloat16 on the way count: a program that leaves them out, or rounds other values in their place, can miss the bound.
Values may be sent and summed in bfloat16 or wider, within the bound.
No kernel may reach another device: no remote copies, remote signals or barrier semaphores. Data moves between devices by JAX's collectives and lax.ppermute only.
A program may use at most 320 MiB of HBM per device.

```python
import jax
import jax.numpy as jnp
from jax import lax

D = 768
HEADS = 12
HEAD_DIM = 64
FF = 2048
VOCAB = 32128
TOK_DEV = 128
SEGS = 4
MEM_DEV = 256
TOKENS = 4096
MEMORY = 8192


def segment_rows(key, count, length):
    pick_key, pad_key = jax.random.split(key)
    quarter = length // 4
    orders = jax.vmap(lambda one_key: jax.random.permutation(one_key, quarter - 1))(jax.random.split(pick_key, count))
    cuts = jnp.sort(orders[:, :SEGS - 1] + 1, axis=1)
    rows = jnp.arange(count).astype(jnp.int32)
    rising = rows * (length // 2) // max(count - 1, 1)
    jitter = jax.random.randint(pad_key, (count,), 0, length // 8 + 1)
    valid = (quarter + rising + jitter)[:, None]
    places = jnp.arange(length)
    marks = 1 + jnp.sum((places[None, :, None] >= cuts[:, None, :]).astype(jnp.int32), axis=2)
    marks = jnp.where(places[None, :] < valid, marks, 0)
    return marks.reshape(count * length).astype(jnp.int32)


def draw_tgt_segments(key, part):
    return segment_rows(jax.random.fold_in(key, 11), TOKENS // TOK_DEV, TOK_DEV)


def draw_mem_segments(key, part):
    return segment_rows(jax.random.fold_in(key, 23), MEMORY // MEM_DEV, MEM_DEV)


def place_ends(values, own_key, low, top_value):
    index_at = [jax.random.randint(jax.random.fold_in(own_key, axis), (), 0, length) for axis, length in enumerate(values.shape)]
    main_axis = values.shape.index(max(values.shape))
    next_to = index_at[:main_axis] + [(index_at[main_axis] + 1) % values.shape[main_axis]] + index_at[main_axis + 1:]
    return values.at[tuple(index_at)].set(low).at[tuple(next_to)].set(top_value)


def shard_levels(rng, dims, cuts, smallest, top_value):
    level, own = 1.0, jax.random.fold_in(rng, 6)
    for axis_at, shards_of in cuts:
        heights = jnp.exp(jax.random.uniform(jax.random.fold_in(own, axis_at), (shards_of,), jnp.float32, smallest / len(cuts), top_value / len(cuts)))
        level = level * jnp.repeat(heights, dims[axis_at] // shards_of).reshape([-1 if axis == axis_at else 1 for axis in range(len(dims))])
    return level


def bell_draw(own_key, extent, deviation, reach, cuts=(), dtype=jnp.bfloat16):
    values = jax.random.normal(own_key, extent, jnp.float32) * deviation
    if len(cuts) > 0:
        values = shard_levels(own_key, extent, cuts, -0.22, 0.18) * values
    return jnp.clip(values, min=-reach, max=reach).astype(dtype)


def setup_inputs(seed: int = 0) -> dict:
    arg_keys = jax.random.split(jax.random.key(seed), 19)
    return {
        "hidden": bell_draw(arg_keys[0], (TOKENS, D), 1.0, 6.0, ((0, 32),)),
        "memory": bell_draw(arg_keys[1], (MEMORY, D), 1.0, 6.0, ((0, 32),)),
        "tgt_segments": draw_tgt_segments(jax.random.fold_in(arg_keys[18], 71), 0),
        "mem_segments": draw_mem_segments(jax.random.fold_in(arg_keys[18], 71), 0),
        "labels": place_ends(jax.random.randint(arg_keys[4], (TOKENS,), 0, VOCAB), jax.random.fold_in(arg_keys[4], 1), 0, VOCAB - 1).astype(jnp.int32),
        "self_query": bell_draw(arg_keys[5], (D, D), (4 * D) ** -0.5, 0.109375, ((0, 8), (1, 4))),
        "self_key": bell_draw(arg_keys[6], (D, D), (4 * D) ** -0.5, 0.109375, ((0, 8), (1, 4))),
        "self_value": bell_draw(arg_keys[7], (D, D), D ** -0.5, 0.21875, ((0, 8), (1, 4))),
        "self_out": bell_draw(arg_keys[8], (D, D), (D // 16) ** -0.5, 0.875, ((0, 8), (1, 4))),
        "cross_query": bell_draw(arg_keys[9], (D, D), (4 * D) ** -0.5, 0.109375, ((0, 8), (1, 4))),
        "cross_key": bell_draw(arg_keys[10], (D, D), (4 * D) ** -0.5, 0.109375, ((0, 8), (1, 4))),
        "cross_value": bell_draw(arg_keys[11], (D, D), D ** -0.5, 0.21875, ((0, 8), (1, 4))),
        "cross_out": bell_draw(arg_keys[12], (D, D), (D // 16) ** -0.5, 0.875, ((0, 8), (1, 4))),
        "gate_weight": bell_draw(arg_keys[13], (D, FF), D ** -0.5, 0.21875, ((0, 8), (1, 4))),
        "up_weight": bell_draw(arg_keys[14], (D, FF), D ** -0.5, 0.21875, ((0, 8), (1, 4))),
        "down_weight": bell_draw(arg_keys[15], (FF, D), (FF // 4) ** -0.5, 0.25, ((0, 8), (1, 4))),
        "norm_gains": jnp.clip(1.0 + 0.1 * jax.random.normal(arg_keys[16], (4 * D,), jnp.float32), 0.5, 1.5).astype(jnp.bfloat16),
        "embedding": bell_draw(arg_keys[17], (VOCAB, D), 2.0, 12.0, ((0, 8), (1, 4))),
    }


EPS = 1e-06
NEG = -1e+30

@jax.custom_vjp
def low(v):
    return lax.optimization_barrier(v.astype(jnp.bfloat16)).astype(jnp.float32)

@jax.custom_vjp
def low_back(v):
    return v

def low_keep(v):
    return (low(v), None)

def low_pass(kept, grad):
    return (grad,)

def back_keep(v):
    return (v, None)

def back_low(kept, grad):
    return (low(grad),)
low.defvjp(low_keep, low_pass)
low_back.defvjp(back_keep, back_low)

def product(left, right):
    return jnp.dot(left, right, precision=lax.Precision.HIGHEST, preferred_element_type=jnp.float32)

def project(left, right):
    return low_back(low(product(left, right)))

def normalize(values):
    return values * lax.rsqrt(lax.optimization_barrier(jnp.mean(values * values, axis=-1, keepdims=True)) + EPS)

def split_heads(values):
    return values.reshape(values.shape[0], HEADS, HEAD_DIM)

def attend(query, keys, values, mask):
    scores = low_back(jnp.einsum('thd,shd->hts', split_heads(query), split_heads(keys), precision=lax.Precision.HIGHEST))
    masked = jnp.where(mask[None], scores, NEG)
    top = lax.optimization_barrier(jnp.max(masked, axis=-1, keepdims=True))
    raised = jnp.exp(masked - top)
    shares = low(raised / lax.optimization_barrier(jnp.sum(raised, axis=-1, keepdims=True)))
    mixed = jnp.einsum('hts,shd->thd', shares, split_heads(values), precision=lax.Precision.HIGHEST)
    return low_back(low(mixed.reshape(query.shape[0], HEADS * HEAD_DIM)))

def layer_row(inputs, memory, target_marks, memory_marks, targets, params):
    near_query, near_key, near_value, near_output, far_query, far_key, far_value, far_output, gate_weight, up_weight, down_weight, gains, table = params
    gains = gains.reshape(4, D)
    places = jnp.arange(target_marks.shape[0])
    self_mask = (target_marks[:, None] == target_marks[None, :]) & (places[None, :] <= places[:, None])
    cross_mask = (target_marks[:, None] == memory_marks[None, :]) | (target_marks[:, None] == 0)
    valid = (target_marks > 0).astype(jnp.float32)
    first_normed = low(normalize(inputs) * gains[0])
    queries = project(first_normed, near_query)
    keys = project(first_normed, near_key)
    values = project(first_normed, near_value)
    attended = attend(queries, keys, values, self_mask)
    after_self = inputs + low_back(product(attended, near_output))
    second_normed = low(normalize(after_self) * gains[1])
    asked = project(second_normed, far_query)
    memory_keys = project(memory, far_key)
    memory_values = project(memory, far_value)
    recalled = attend(asked, memory_keys, memory_values, cross_mask)
    after_cross = after_self + low_back(product(recalled, far_output))
    third_normed = low(normalize(after_cross) * gains[2])
    gate_rows = low_back(product(third_normed, gate_weight))
    up_rows = low_back(product(third_normed, up_weight))
    activated = low(jax.nn.gelu(gate_rows, approximate=True) * up_rows)
    block_sum = after_cross + low_back(product(activated, down_weight))
    exit_rows = low(normalize(block_sum) * gains[3] * D ** (-0.5))
    logits = low_back(product(exit_rows, table.T))
    top = lax.optimization_barrier(jnp.max(logits, axis=1, keepdims=True))
    normalizer = top + jnp.log(lax.optimization_barrier(jnp.sum(jnp.exp(logits - top), axis=1, keepdims=True)))
    onehot = (jnp.arange(VOCAB)[None, :] == targets[:, None]).astype(jnp.float32)
    picked = lax.optimization_barrier(jnp.sum(onehot * logits, axis=1))
    return (block_sum, jnp.sum((normalizer[:, 0] - picked) * valid))

def forward(inputs, memory, params, target_marks, memory_marks, targets):
    count = inputs.shape[0] // TOK_DEV
    items = (inputs.reshape(count, TOK_DEV, D), memory.reshape(count, MEM_DEV, D), target_marks.reshape(count, TOK_DEV), memory_marks.reshape(count, MEM_DEV), targets.reshape(count, TOK_DEV))
    checked = jax.checkpoint(layer_row)

    def advance(total, item):
        block_rows, part_loss = checked(item[0], item[1], item[2], item[3], item[4], params)
        return (total + part_loss, block_rows)
    total, blocks = lax.scan(advance, jnp.zeros((), jnp.float32), items)
    return (blocks.reshape(count * TOK_DEV, D), total)

def reference(hidden, memory, tgt_segments, mem_segments, labels, self_query, self_key, self_value, self_out, cross_query, cross_key, cross_value, cross_out, gate_weight, up_weight, down_weight, norm_gains, embedding):
    params = tuple((weight.astype(jnp.float32) for weight in (self_query, self_key, self_value, self_out, cross_query, cross_key, cross_value, cross_out, gate_weight, up_weight, down_weight, norm_gains, embedding)))

    def whole(inputs, encoded, weights):
        return forward(inputs, encoded, weights, tgt_segments, mem_segments, labels)
    (block, total), pull = jax.vjp(whole, hidden.astype(jnp.float32), memory.astype(jnp.float32), params)
    grad_inputs, grad_encoded, grads = pull((jnp.zeros_like(block), jnp.ones_like(total)))
    return (block.astype(jnp.bfloat16), total / TOKENS, grad_inputs, grad_encoded, grads[0], grads[1], grads[2], grads[3], grads[4], grads[5], grads[6], grads[7], grads[8], grads[9], grads[10], grads[11], grads[12])
```

```python
import jax
import jax.numpy as jnp
from jax import lax
from jax.sharding import PartitionSpec as P

D = 768
HEADS = 12
HEAD_DIM = 64


EPS = 1e-06
NEG = -1e30


def normalize(values):
    return values * lax.rsqrt(jnp.mean(values * values, axis=-1, keepdims=True) + EPS)


def norm_back(values, gain, grad, factor):

    def scaled(inner, weight):
        return normalize(inner) * weight * factor

    _, pull = jax.vjp(scaled, values, gain)
    return pull(grad)


def matmul(left, right):
    return jnp.dot(left, right, preferred_element_type=jnp.float32)


def times_transposed(left, right):
    return lax.dot_general(
        left, right, (((1,), (1,)), ((), ())), preferred_element_type=jnp.float32
    )


def transposed_times(left, right):
    return lax.dot_general(
        left, right, (((0,), (0,)), ((), ())), preferred_element_type=jnp.float32
    )


def split_heads(values):
    return values.reshape(values.shape[0], HEADS, HEAD_DIM)


def join_heads(values):
    return values.reshape(values.shape[0], HEADS * HEAD_DIM)


def masked_scores(query, keys, mask):
    scores = jnp.einsum(
        "thd,shd->hts", split_heads(query), split_heads(keys), preferred_element_type=jnp.float32
    )
    return jnp.where(mask[None], scores, NEG)


def attend(query, keys, values, mask):
    scores = masked_scores(query, keys, mask)
    top = jnp.max(scores, axis=-1, keepdims=True)
    normalizer = top + jnp.log(jnp.sum(jnp.exp(scores - top), axis=-1, keepdims=True))
    shares = jnp.exp(scores - normalizer).astype(jnp.bfloat16)
    mixed = jnp.einsum(
        "hts,shd->thd", shares, split_heads(values), preferred_element_type=jnp.float32
    )
    return (join_heads(mixed).astype(jnp.bfloat16), normalizer)


def attend_back(query, keys, values, mask, normalizer, out_grad):
    shares = jnp.exp(masked_scores(query, keys, mask) - normalizer)
    heads_grad = split_heads(out_grad)
    share_grad = jnp.einsum(
        "thd,shd->hts", heads_grad, split_heads(values), preferred_element_type=jnp.float32
    )
    inner = jnp.sum(shares * share_grad, axis=-1, keepdims=True)
    score_grad = (shares * (share_grad - inner)).astype(jnp.bfloat16)
    query_grad = jnp.einsum(
        "hts,shd->thd", score_grad, split_heads(keys), preferred_element_type=jnp.float32
    )
    key_grad = jnp.einsum(
        "hts,thd->shd", score_grad, split_heads(query), preferred_element_type=jnp.float32
    )
    value_grad = jnp.einsum(
        "hts,thd->shd", shares.astype(jnp.bfloat16), heads_grad, preferred_element_type=jnp.float32
    )
    return (
        join_heads(query_grad).astype(jnp.bfloat16),
        join_heads(key_grad).astype(jnp.bfloat16),
        join_heads(value_grad).astype(jnp.bfloat16),
    )


def swap(value, axis, step):
    size = lax.axis_size(axis)
    return lax.ppermute(value, axis, [(place, place ^ step) for place in range(size)])


def relative_order(size):
    order, step = [0], size // 2
    while step:
        order = order + [place | step for place in order]
        step //= 2
    return order


def gather_relative(value, axis):
    stack, step = value[None], lax.axis_size(axis) // 2
    while step:
        stack = jnp.concatenate([stack, swap(stack, axis, step)], axis=0)
        step //= 2
    return stack


def exchange_relative(blocks, axis):
    me = lax.axis_index(axis)
    got = []
    for step in relative_order(lax.axis_size(axis)):
        block = lax.dynamic_index_in_dim(blocks, me ^ step, 0, keepdims=False)
        got.append(block if step == 0 else swap(block, axis, step))
    return jnp.stack(got)


def column_blocks(values, count):
    rows, width = values.shape
    return values.reshape(rows, count, width // count).transpose(1, 0, 2)


def flat_rows(stack):
    return stack.reshape(stack.shape[0] * stack.shape[1], stack.shape[2])


def body(
    hidden,
    memory,
    tgt_segments,
    mem_segments,
    labels,
    self_query,
    self_key,
    self_value,
    self_out,
    cross_query,
    cross_key,
    cross_value,
    cross_out,
    gate_weight,
    up_weight,
    down_weight,
    norm_gains,
    embedding,
):
    wide, deep = lax.axis_size("dp"), lax.axis_size("fsdp")
    rows, cols = self_query.shape
    ff_cols, ff_rows = gate_weight.shape[1], down_weight.shape[0]
    ff = ff_cols * wide
    folds = cols // rows
    gain_column = jnp.zeros((rows, 128), jnp.bfloat16).at[: norm_gains.shape[0], 0].set(norm_gains)
    down_turned = down_weight.T.reshape(folds, rows, ff_rows).transpose(1, 0, 2)
    pack = jnp.concatenate(
        [
            self_query,
            self_key,
            self_value,
            self_out,
            cross_query,
            cross_key,
            cross_value,
            cross_out,
            gate_weight,
            up_weight,
            down_turned.reshape(rows, folds * ff_rows),
            gain_column,
        ],
        axis=1,
    )
    gathered = lax.all_gather(pack, ("dp", "fsdp"), axis=0, tiled=True)
    gathered = gathered.reshape(wide, deep * rows, pack.shape[1])
    table = lax.all_gather(embedding, "dp", axis=1, tiled=True)

    def columns_of(start, width):
        return gathered[:, :, start : start + width].transpose(1, 0, 2).reshape(D, wide * width)

    squares = [columns_of(index * cols, cols) for index in range(8)]
    query_full, key_full, value_full, output_full = squares[:4]
    recall_query, recall_key, recall_value, recall_output = squares[4:]
    at = 8 * cols
    gate_full = columns_of(at, ff_cols)
    up_full = columns_of(at + ff_cols, ff_cols)
    at = at + 2 * ff_cols
    down_turned = (
        gathered[:, :, at : at + folds * ff_rows]
        .reshape(wide, deep, rows, folds, ff_rows)
        .transpose(0, 3, 2, 1, 4)
        .reshape(D, ff)
    )
    at = at + folds * ff_rows
    gains = gathered[:, :, at].reshape(wide, deep, rows)[:, :, : norm_gains.shape[0]]
    gains = gains.astype(jnp.float32).reshape(4, D)

    inputs = hidden.astype(jnp.float32)
    length = hidden.shape[0]
    places = jnp.arange(length)
    self_mask = (tgt_segments[:, None] == tgt_segments[None, :]) & (
        places[None, :] <= places[:, None]
    )
    cross_mask = (tgt_segments[:, None] == mem_segments[None, :]) | (tgt_segments[:, None] == 0)
    valid = (tgt_segments > 0).astype(jnp.int32)
    group_marks = lax.all_gather(jnp.stack([labels, valid]), "fsdp", axis=1, tiled=True)
    group_labels, group_valid = group_marks[0], group_marks[1].astype(jnp.float32)
    memory_near = flat_rows(gather_relative(memory, "dp"))

    first_normed = (normalize(inputs) * gains[0]).astype(jnp.bfloat16)
    queries = matmul(first_normed, query_full).astype(jnp.bfloat16)
    keys = matmul(first_normed, key_full).astype(jnp.bfloat16)
    values = matmul(first_normed, value_full).astype(jnp.bfloat16)
    attended, self_norms = attend(queries, keys, values, self_mask)
    after_self = inputs + matmul(attended, output_full)
    second_normed = (normalize(after_self) * gains[1]).astype(jnp.bfloat16)
    asked = matmul(second_normed, recall_query).astype(jnp.bfloat16)
    memory_keys = matmul(memory, recall_key).astype(jnp.bfloat16)
    memory_values = matmul(memory, recall_value).astype(jnp.bfloat16)
    recalled, cross_norms = attend(asked, memory_keys, memory_values, cross_mask)
    after_cross = after_self + matmul(recalled, recall_output)
    third_normed = (normalize(after_cross) * gains[2]).astype(jnp.bfloat16)
    gate_rows = matmul(third_normed, gate_full)
    up_rows = matmul(third_normed, up_full)
    activated = (jax.nn.gelu(gate_rows, approximate=True) * up_rows).astype(jnp.bfloat16)
    block_sum = after_cross + times_transposed(activated, down_turned)
    exit_rows = (normalize(block_sum) * gains[3] * D ** (-0.5)).astype(jnp.bfloat16)

    group_exit = lax.all_gather(exit_rows, "fsdp", axis=0, tiled=True)
    factors = jnp.concatenate(
        [first_normed, attended, second_normed, recalled, third_normed, activated], axis=1
    )
    near = flat_rows(gather_relative(factors, "dp"))
    first_near = near[:, :D]
    attended_near = near[:, D : 2 * D]
    second_near = near[:, 2 * D : 3 * D]
    recalled_near = near[:, 3 * D : 4 * D]
    third_near = near[:, 4 * D : 5 * D]
    activated_near = near[:, 5 * D :]

    logits = times_transposed(group_exit, table)
    vocab = table.shape[0]
    first_entry = lax.axis_index("fsdp") * vocab
    onehot = (
        jnp.arange(vocab)[None, :] == (group_labels - first_entry)[:, None]
    ).astype(jnp.float32)
    top = jnp.max(logits, axis=1)
    raised = jnp.sum(jnp.exp(logits - top[:, None]), axis=1)
    picked = jnp.sum(onehot * logits, axis=1)
    stats = lax.all_gather(jnp.stack([top, raised, picked]), "fsdp", axis=0, tiled=False)
    top = jnp.max(stats[:, 0], axis=0)
    normalizer = top + jnp.log(jnp.sum(stats[:, 1] * jnp.exp(stats[:, 0] - top), axis=0))
    group_loss = jnp.sum((normalizer - jnp.sum(stats[:, 2], axis=0)) * group_valid)
    logit_grad = (
        (jnp.exp(logits - normalizer[:, None]) - onehot) * group_valid[:, None]
    ).astype(jnp.bfloat16)
    exit_grad = lax.psum_scatter(
        matmul(logit_grad, table).astype(jnp.bfloat16), "fsdp", scatter_dimension=0, tiled=True
    ).astype(jnp.float32)
    grad_embedding = lax.psum_scatter(
        transposed_times(logit_grad, group_exit).astype(jnp.bfloat16),
        "dp",
        scatter_dimension=1,
        tiled=True,
    ).astype(jnp.float32)

    block_grad, exit_gain = norm_back(block_sum, gains[3], exit_grad, D ** (-0.5))
    down_input = block_grad.astype(jnp.bfloat16)
    act_grad = matmul(down_input, down_turned)
    _, pull = jax.vjp(
        lambda gate_in, up_in: jax.nn.gelu(gate_in, approximate=True) * up_in, gate_rows, up_rows
    )
    gate_grad, up_grad = pull(act_grad)
    gate_grad = gate_grad.astype(jnp.bfloat16)
    up_grad = up_grad.astype(jnp.bfloat16)

    def share(*grads):
        blocks = jnp.concatenate([column_blocks(grad, wide) for grad in grads], axis=2)
        got = flat_rows(exchange_relative(blocks, "dp"))
        parts, at = [], 0
        for grad in grads:
            width = grad.shape[1] // wide
            parts.append(got[:, at : at + width])
            at += width
        return parts

    gate_near, up_near, down_near = share(gate_grad, up_grad, down_input)
    grad_gate = transposed_times(third_near, gate_near)
    grad_up = transposed_times(third_near, up_near)
    grad_down = transposed_times(down_near, activated_near)
    grad_down = (
        grad_down.reshape(folds, rows, deep, ff_rows)
        .transpose(2, 1, 0, 3)
        .reshape(D, folds * ff_rows)
    )
    ff_grads = lax.psum_scatter(
        jnp.concatenate([grad_gate, grad_up, grad_down], axis=1).astype(jnp.bfloat16),
        "fsdp",
        scatter_dimension=0,
        tiled=True,
    )

    third_grad = times_transposed(gate_grad, gate_full) + times_transposed(up_grad, up_full)
    cross_back, third_gain = norm_back(after_cross, gains[2], third_grad, 1.0)
    after_cross_grad = block_grad + cross_back
    cross_branch = after_cross_grad.astype(jnp.bfloat16)
    recalled_grad = times_transposed(cross_branch, recall_output).astype(jnp.bfloat16)
    probe_grad, lookup_grad, content_grad = attend_back(
        asked, memory_keys, memory_values, cross_mask, cross_norms, recalled_grad
    )
    grad_memory = times_transposed(lookup_grad, recall_key) + times_transposed(
        content_grad, recall_value
    )
    second_grad = times_transposed(probe_grad, recall_query)
    self_back, second_gain = norm_back(after_self, gains[1], second_grad, 1.0)
    after_self_grad = after_cross_grad + self_back
    self_branch = after_self_grad.astype(jnp.bfloat16)
    cross_near, probe_near = share(cross_branch, probe_grad)
    lookup_near, content_near = share(lookup_grad, content_grad)
    attended_grad = times_transposed(self_branch, output_full).astype(jnp.bfloat16)
    query_grad, key_grad, value_grad = attend_back(
        queries, keys, values, self_mask, self_norms, attended_grad
    )
    self_near, query_near, key_near, value_near = share(
        self_branch, query_grad, key_grad, value_grad
    )
    square_grads = lax.psum_scatter(
        jnp.concatenate(
            [
                transposed_times(first_near, query_near),
                transposed_times(first_near, key_near),
                transposed_times(first_near, value_near),
                transposed_times(attended_near, self_near),
                transposed_times(second_near, probe_near),
                transposed_times(memory_near, lookup_near),
                transposed_times(memory_near, content_near),
                transposed_times(recalled_near, cross_near),
            ],
            axis=1,
        ).astype(jnp.bfloat16),
        "fsdp",
        scatter_dimension=0,
        tiled=True,
    )
    first_grad = (
        times_transposed(query_grad, query_full)
        + times_transposed(key_grad, key_full)
        + times_transposed(value_grad, value_full)
    )
    input_back, first_gain = norm_back(inputs, gains[0], first_grad, 1.0)
    grad_hidden = after_self_grad + input_back

    owned = [
        square_grads[:, index * cols : (index + 1) * cols].astype(jnp.float32)
        for index in range(8)
    ]
    owned.append(ff_grads[:, :ff_cols].astype(jnp.float32))
    owned.append(ff_grads[:, ff_cols : 2 * ff_cols].astype(jnp.float32))
    owned.append(
        ff_grads[:, 2 * ff_cols :]
        .reshape(rows, folds, ff_rows)
        .transpose(1, 0, 2)
        .reshape(cols, ff_rows)
        .T.astype(jnp.float32)
    )
    gain_grad = lax.psum_scatter(
        jnp.concatenate([first_gain, second_gain, third_gain, exit_gain]),
        ("dp", "fsdp"),
        scatter_dimension=0,
        tiled=True,
    )
    loss_total = lax.psum(group_loss, "dp")
    loss_mean = loss_total / (length * wide * deep)
    return (
        block_sum.astype(jnp.bfloat16),
        loss_mean,
        grad_hidden,
        grad_memory,
        *owned,
        gain_grad,
        grad_embedding,
    )


def solution(mesh):
    in_specs = (
        P(("dp", "fsdp"), None),
        P(("dp", "fsdp"), None),
        P(("dp", "fsdp")),
        P(("dp", "fsdp")),
        P(("dp", "fsdp")),
        P("fsdp", "dp"),
        P("fsdp", "dp"),
        P("fsdp", "dp"),
        P("fsdp", "dp"),
        P("fsdp", "dp"),
        P("fsdp", "dp"),
        P("fsdp", "dp"),
        P("fsdp", "dp"),
        P("fsdp", "dp"),
        P("fsdp", "dp"),
        P("fsdp", "dp"),
        P(("dp", "fsdp")),
        P("fsdp", "dp"),
    )
    out_specs = (
        P(("dp", "fsdp"), None),
        P(),
        P(("dp", "fsdp"), None),
        P(("dp", "fsdp"), None),
        P("fsdp", "dp"),
        P("fsdp", "dp"),
        P("fsdp", "dp"),
        P("fsdp", "dp"),
        P("fsdp", "dp"),
        P("fsdp", "dp"),
        P("fsdp", "dp"),
        P("fsdp", "dp"),
        P("fsdp", "dp"),
        P("fsdp", "dp"),
        P("fsdp", "dp"),
        P(("dp", "fsdp")),
        P("fsdp", "dp"),
    )
    return jax.shard_map(body, mesh=mesh, in_specs=in_specs, out_specs=out_specs, check_vma=False)
```
